32 devices in a mesh: frame: 8 (over y, x, core), tensor: 4 (over z).
Axes of the slice: x: 2, y: 2, z: 4, core: 2. Of those that a mesh axis runs over, the one named last changes fastest.
Arguments:
- hidden: bfloat16 [8192, 3072], P(('frame', 'tensor')), may hold values from -6 to 6
- qkv_weight: bfloat16 [3072, 3, 3072], P(None, None, 'tensor'), may hold values from -0.109375 to 0.109375
- norm_gain: float32 [2, 128], replicated, may hold values from 0.5 to 10, as said below
- out_grad: bfloat16 [8192, 3072], P('frame', 'tensor'), may hold values from -0.15625 to 0.15625
Outputs:
- attended: bfloat16 [8192, 3072], P('frame', 'tensor')
- weight_grad: float32 [3072, 3, 3072], P('frame', None, 'tensor')
The draws below stay inside these ranges and needn't reach their ends.
Inputs may be any that keep to these rules, and one draw needn't show every extreme that they name: `norm_gain`: every gain is positive.
All inputs are finite; a program needn't handle non-finite values.
Results may differ from the reference program's by a relative error of at most 0.028.
The reference program's roundings to bfloat16 on the way (of `weights`, `score_grads` and `qkv_grad`) count: a program that leaves them out, or rounds other values in their place, can miss the bound.
Values may be sent and summed in bfloat16 or wider, within the bound.
A program may use at most 192 MiB of HBM per device.

```python
import math
import jax
import jax.numpy as jnp
from jax import lax

HEAD_DIM = 128
D = 3072
GROUP = 1024
TOKENS = 8192
N_FRAME = 8


def draw_norm_gain(key, part):
    return jnp.exp(jax.random.uniform(key, (2, HEAD_DIM), jnp.float32, math.log(0.6), math.log(1.8)))


def strengthened(values, stream_key, source, target, parts, factor):
    def block_of(dim):
        return (jnp.arange(values.shape[dim]) // (values.shape[dim] // parts)).reshape((-1,) + (1,) * (values.ndim - 1 - dim))

    first = jax.random.permutation(stream_key, parts)[block_of(target)]
    far = (block_of(target) + parts // 2) % parts
    return jnp.where((block_of(source) == first) | (block_of(source) == far), factor * values, values)


def shard_levels(rng, extent, pieces, least, high):
    def one(position, parts):
        draws = jax.random.uniform(jax.random.fold_in(jax.random.fold_in(rng, 6), position), (parts,), jnp.float32, least / len(pieces), high / len(pieces))
        return jnp.repeat(jnp.exp(draws), extent[position] // parts).reshape((-1,) + (1,) * (len(extent) - position - 1))

    loudness = one(*pieces[0])
    for cut in pieces[1:]:
        loudness = loudness * one(*cut)
    return loudness


def gaussian(stream_key, extent, spread, most, cuts=(), kind=jnp.bfloat16):
    result = spread * jax.random.normal(stream_key, extent, jnp.float32)
    if cuts:
        result = result * shard_levels(stream_key, extent, cuts, -0.22, 0.18)
    return jnp.clip(result, -most, most).astype(kind)


def noise_with(key, shape, scale, limit, pieces, heavy, held_as=jnp.bfloat16):
    drawn = scale * jax.random.normal(key, shape, jnp.float32)
    if pieces:
        drawn = drawn * shard_levels(key, shape, pieces, -0.22, 0.18)
    return jnp.clip(strengthened(drawn, jax.random.fold_in(key, 3), *heavy), -limit, limit).astype(held_as)


def setup_inputs(seed: int = 0) -> dict:
    seeds = jax.random.split(jax.random.key(seed), 5)
    hidden = noise_with(seeds[0], (TOKENS, D), 1.0, 6.0, ((0, 32),), (0, 1, 32, 2.75))
    qkv_weight = gaussian(seeds[1], (D, 3, D), D ** -0.5, 0.109375, ((2, 4),))
    norm_gain = draw_norm_gain(jax.random.fold_in(seeds[4], 71), 0)
    out_grad = gaussian(seeds[3], (TOKENS, D), (TOKENS ** -0.5), 0.15625, ((0, 8), (1, 4)))
    return dict(hidden=hidden, qkv_weight=qkv_weight, norm_gain=norm_gain, out_grad=out_grad)


EPSILON = 1e-06

def norm_heads(projected, gain):
    inverse_rms = lax.rsqrt(lax.optimization_barrier(jnp.mean(projected * projected, axis=-1, keepdims=True)) + EPSILON)
    return (projected * inverse_rms * gain, inverse_rms)

def norm_back(projected, inverse_rms, gain, grad):
    weighted = grad * gain
    inner = lax.optimization_barrier(jnp.mean(projected * weighted, axis=-1, keepdims=True))
    return inverse_rms * weighted - projected * (inverse_rms * inverse_rms * inverse_rms) * inner

def product(form, left, right):
    return jnp.einsum(form, left.astype(jnp.float32), right.astype(jnp.float32))

def window_attention(query, window, out_grad, valid):
    total_rows = query.shape[0]
    block = min(512, total_rows)
    keys = window[:, 0]
    values = window[:, 1]
    factor = query.shape[-1] ** (-0.5)
    output_list = []
    query_grads = []
    keyval_grad = jnp.zeros(window.shape, jnp.float32)
    for first_row in range(0, total_rows, block):
        query_block = query[first_row:first_row + block]
        grad_block = out_grad[first_row:first_row + block]
        scores = product('qhd,khd->hqk', query_block, keys) * factor
        scores = jnp.where(valid[None, None, :], scores, -1e+30)
        peak = lax.optimization_barrier(jnp.max(scores, axis=-1, keepdims=True))
        raised = jnp.exp(scores - peak)
        weights = (raised / lax.optimization_barrier(jnp.sum(raised, axis=-1, keepdims=True))).astype(jnp.bfloat16)
        attended = product('hqk,khd->qhd', weights, values).astype(jnp.bfloat16)
        row_dots = lax.optimization_barrier(jnp.sum(grad_block.astype(jnp.float32) * attended.astype(jnp.float32), axis=-1))
        prob_grads = product('qhd,khd->hqk', grad_block, values)
        score_grads = (weights.astype(jnp.float32) * (prob_grads - row_dots.T[:, :, None])).astype(jnp.bfloat16)
        query_grad = product('hqk,khd->qhd', score_grads, keys) * factor
        key_grad = product('hqk,qhd->khd', score_grads, query_block) * factor
        value_grad = product('hqk,qhd->khd', weights, grad_block)
        keyval_grad = keyval_grad + jnp.stack([key_grad, value_grad], axis=1)
        output_list.append(attended)
        query_grads.append(query_grad)
    return (jnp.concatenate(output_list, 0), jnp.concatenate(query_grads, 0), keyval_grad)

def reference(hidden, qkv_weight, norm_gain, out_grad):
    tokens, width = hidden.shape
    heads = width // HEAD_DIM
    projected = jnp.dot(hidden, qkv_weight.reshape(width, 3 * width), preferred_element_type=jnp.float32)
    projected = projected.reshape(tokens, 3, heads, HEAD_DIM)
    query_normed, query_rms = norm_heads(projected[:, 0], norm_gain[0])
    key_normed, key_rms = norm_heads(projected[:, 1], norm_gain[1])
    query = query_normed.astype(jnp.bfloat16)
    keyval = jnp.stack([key_normed.astype(jnp.bfloat16), projected[:, 2].astype(jnp.bfloat16)], 1)
    half = GROUP // 2
    padded = jnp.pad(keyval, ((half, half), (0, 0), (0, 0), (0, 0)))
    grads_heads = out_grad.reshape(tokens, heads, HEAD_DIM)

    def one_group(group_index):
        start = (group_index * GROUP).astype(jnp.int32)
        window = lax.dynamic_slice_in_dim(padded, start, 2 * GROUP, 0)
        query_rows = lax.dynamic_slice_in_dim(query, start, GROUP, 0)
        grad_rows = lax.dynamic_slice_in_dim(grads_heads, start, GROUP, 0)
        place = start + jnp.arange(2 * GROUP, dtype=jnp.int32)
        valid = (place >= half) & (place < tokens + half)
        return window_attention(query_rows, window, grad_rows, valid)
    outputs, query_grads, keyval_grads = lax.map(one_group, jnp.arange(N_FRAME, dtype=jnp.int32))
    lower = keyval_grads[:, :half]
    own = keyval_grads[:, half:half + GROUP]
    upper = keyval_grads[:, half + GROUP:]
    zero_rows = jnp.zeros_like(lower[:1])
    from_prev = jnp.concatenate([zero_rows, upper[:-1]], 0)
    from_next = jnp.concatenate([lower[1:], zero_rows], 0)
    keyval_grad = (own + jnp.concatenate([from_prev, from_next], 1)).reshape(tokens, 2, heads, HEAD_DIM)
    query_grad = query_grads.reshape(tokens, heads, HEAD_DIM)
    query_raw_grad = norm_back(projected[:, 0], query_rms, norm_gain[0], query_grad)
    key_raw_grad = norm_back(projected[:, 1], key_rms, norm_gain[1], keyval_grad[:, 0])
    qkv_grad = jnp.stack([query_raw_grad, key_raw_grad, keyval_grad[:, 1]], 1).astype(jnp.bfloat16)
    qkv_grad = qkv_grad.reshape(tokens, 3 * width)
    weight_grad = jnp.dot(hidden.T, qkv_grad, preferred_element_type=jnp.float32).reshape(width, 3, width)
    return (outputs.reshape(tokens, width), weight_grad)
```

```python
import functools
import math

import jax
import jax.numpy as jnp
from jax import lax
from jax.experimental import pallas as pl
from jax.experimental.pallas import tpu as pltpu
from jax.sharding import PartitionSpec as P

HEAD_DIM = 128
EPSILON = 1e-06
MASKED = -1e30
NT = (((1,), (1,)), ((), ()))


def ppermute_by(value, axis, steps):
    count = lax.axis_size(axis)
    initial, last = (max(0, -steps), min(count, count - steps))
    return lax.ppermute(value, axis, [(source, source + steps) for source in range(initial, last)])


def inverse_rms_of(raw):
    return lax.rsqrt(jnp.mean(raw * raw, axis=-1, keepdims=True) + EPSILON)


def norm_back(raw, inverse_rms, gain, grad):
    weighted = grad * gain
    inner = jnp.mean(raw * weighted, axis=-1, keepdims=True)
    return inverse_rms * weighted - raw * (inverse_rms * inverse_rms * inverse_rms) * inner


def dot32(left, right):
    return jnp.dot(left, right, preferred_element_type=jnp.float32)


def dot_nt(left, right):
    return lax.dot_general(left, right, NT, preferred_element_type=jnp.float32)


def key_norm_kernel(raw_ref, gain_ref, out_ref):
    raw = raw_ref[...]
    out_ref[...] = (raw * inverse_rms_of(raw) * gain_ref[1:2]).astype(out_ref.dtype)


def key_norm(raw, gain):
    rows, local = raw.shape
    spec = pl.BlockSpec((rows, HEAD_DIM), lambda h: (0, h))
    return pl.pallas_call(
        key_norm_kernel,
        grid=(local // HEAD_DIM,),
        in_specs=[spec, pl.BlockSpec(gain.shape, lambda h: (0, 0))],
        out_specs=spec,
        out_shape=jax.ShapeDtypeStruct(raw.shape, jnp.bfloat16),
        name="key_norm",
    )(raw, gain)


def key_back_kernel(dk_ref, dv_ref, pk_ref, pv_ref, nk_ref, nv_ref, raw_ref, gain_ref, kout_ref, vout_ref):
    half = pk_ref.shape[0]
    gain = gain_ref[1:2]
    for part, (k_edge, v_edge) in enumerate(((pk_ref, pv_ref), (nk_ref, nv_ref))):
        rows = pl.ds(part * half, half)
        raw = raw_ref[rows]
        grad = dk_ref[rows] + k_edge[...].astype(jnp.float32)
        kout_ref[rows] = norm_back(raw, inverse_rms_of(raw), gain, grad).astype(jnp.bfloat16)
        vout_ref[rows] = (dv_ref[rows] + v_edge[...].astype(jnp.float32)).astype(jnp.bfloat16)


def key_back(dk, dv, pk, pv, nk, nv, raw, gain):
    rows, local = dk.shape
    spec = pl.BlockSpec((rows, HEAD_DIM), lambda h: (0, h))
    edge = pl.BlockSpec((pk.shape[0], HEAD_DIM), lambda h: (0, h))
    shape = jax.ShapeDtypeStruct(dk.shape, jnp.bfloat16)
    return pl.pallas_call(
        key_back_kernel,
        grid=(local // HEAD_DIM,),
        in_specs=[spec, spec, edge, edge, edge, edge, spec, pl.BlockSpec(gain.shape, lambda h: (0, 0))],
        out_specs=(spec, spec),
        out_shape=(shape, shape),
        name="key_back",
    )(dk, dv, pk, pv, nk, nv, raw, gain)


def attend_kernel(
    bias_ref, gain_ref, raw_ref, grad_ref, kp_ref, ko_ref, kn_ref, vp_ref, vo_ref, vn_ref,
    att_ref, qpart_ref, dk_ref, dv_ref, dkp_ref, dvp_ref, dkn_ref, dvn_ref,
    kt, vt, score, prob_grad, weight, score_grad, dk_acc, dv_acc,
):
    half = kp_ref.shape[0]
    total = dk_acc.shape[0]
    step, last = pl.program_id(1), pl.num_programs(1) - 1
    factor = HEAD_DIM ** (-0.5)
    chunks = [
        (kp_ref, vp_ref, slice(0, half), bias_ref[0]),
        (ko_ref, vo_ref, slice(0, half), None),
        (ko_ref, vo_ref, slice(half, 2 * half), None),
        (kn_ref, vn_ref, slice(0, half), bias_ref[1]),
    ]

    @pl.when(step == 0)
    def _():
        for i, (k_ref, v_ref, rows, _) in enumerate(chunks):
            kt[:, i * half : (i + 1) * half] = k_ref[rows].T
            vt[:, i * half : (i + 1) * half] = v_ref[rows].T
        dk_acc[...] = jnp.zeros_like(dk_acc)
        dv_acc[...] = jnp.zeros_like(dv_acc)

    raw = raw_ref[...]
    gain = gain_ref[0:1]
    inverse_rms = inverse_rms_of(raw)
    query = (raw * inverse_rms * gain).astype(jnp.bfloat16)
    grad = grad_ref[...]
    peak = None
    for i, (k_ref, v_ref, rows, bias) in enumerate(chunks):
        place = slice(i * half, (i + 1) * half)
        s = dot_nt(k_ref[rows], query)
        if bias is not None:
            s = s + bias
        score[place] = s
        top = jnp.max(s, axis=0, keepdims=True)
        peak = top if peak is None else jnp.maximum(peak, top)
    norm = None
    scale = factor * math.log2(math.e)
    for i, (k_ref, v_ref, rows, _) in enumerate(chunks):
        place = slice(i * half, (i + 1) * half)
        raised = jnp.exp2((score[place] - peak) * scale)
        score[place] = raised
        part = jnp.sum(raised, axis=0, keepdims=True)
        norm = part if norm is None else norm + part
        prob_grad[place] = dot_nt(v_ref[rows], grad)
    inverse = 1.0 / norm
    attended = None
    for i in range(4):
        place = slice(i * half, (i + 1) * half)
        w = (score[place] * inverse).astype(jnp.bfloat16)
        weight[place] = w
        term = dot32(vt[:, place], w)
        attended = term if attended is None else attended + term
        dv_acc[place] += dot32(w, grad)
    attended = attended.T.astype(jnp.bfloat16)
    att_ref[...] = attended
    dots = jnp.sum((grad.astype(jnp.float32) * attended.astype(jnp.float32)).T, axis=0, keepdims=True)
    query_grad = None
    for i in range(4):
        place = slice(i * half, (i + 1) * half)
        ds = (weight[place].astype(jnp.float32) * (prob_grad[place] - dots)).astype(jnp.bfloat16)
        term = dot32(kt[:, place], ds)
        query_grad = term if query_grad is None else query_grad + term
        dk_acc[place] += dot32(ds, query)
    query_grad = query_grad.T * factor
    qpart_ref[...] = norm_back(raw, inverse_rms, gain, query_grad).astype(jnp.bfloat16)

    @pl.when(step == last)
    def _():
        dkp_ref[...] = (dk_acc[0:half] * factor).astype(jnp.bfloat16)
        dvp_ref[...] = dv_acc[0:half].astype(jnp.bfloat16)
        dk_ref[...] = dk_acc[half : 3 * half] * factor
        dv_ref[...] = dv_acc[half : 3 * half]
        dkn_ref[...] = (dk_acc[3 * half : total] * factor).astype(jnp.bfloat16)
        dvn_ref[...] = dv_acc[3 * half : total].astype(jnp.bfloat16)


def attend(bias, gain, raw, grad, kp, ko, kn, vp, vo, vn):
    rows, local = raw.shape
    heads, half = local // HEAD_DIM, rows // 2
    block = min(256, rows)
    by_row = pl.BlockSpec((block, HEAD_DIM), lambda h, j: (j, h))
    own = pl.BlockSpec((rows, HEAD_DIM), lambda h, j: (0, h))
    edge = pl.BlockSpec((half, HEAD_DIM), lambda h, j: (0, h))
    full = jax.ShapeDtypeStruct((rows, local), jnp.bfloat16)
    full32 = jax.ShapeDtypeStruct((rows, local), jnp.float32)
    edge_shape = jax.ShapeDtypeStruct((half, local), jnp.bfloat16)
    window = 2 * rows
    flops = 12 * rows * window * local
    return pl.pallas_call(
        attend_kernel,
        grid=(heads, rows // block),
        in_specs=[
            pl.BlockSpec(memory_space=pltpu.SMEM),
            pl.BlockSpec(gain.shape, lambda h, j: (0, 0)),
            by_row, by_row, edge, own, edge, edge, own, edge,
        ],
        out_specs=(by_row, by_row, own, own, edge, edge, edge, edge),
        out_shape=(full, full, full32, full32, edge_shape, edge_shape, edge_shape, edge_shape),
        scratch_shapes=[
            pltpu.VMEM((HEAD_DIM, window), jnp.bfloat16),
            pltpu.VMEM((HEAD_DIM, window), jnp.bfloat16),
            pltpu.VMEM((window, block), jnp.float32),
            pltpu.VMEM((window, block), jnp.float32),
            pltpu.VMEM((window, block), jnp.bfloat16),
            pltpu.VMEM((window, block), jnp.bfloat16),
            pltpu.VMEM((window, HEAD_DIM), jnp.float32),
            pltpu.VMEM((window, HEAD_DIM), jnp.float32),
        ],
        compiler_params=pltpu.CompilerParams(
            dimension_semantics=("arbitrary", "arbitrary"), vmem_limit_bytes=40 * 1024 * 1024
        ),
        cost_estimate=pl.CostEstimate(
            flops=flops, bytes_accessed=16 * rows * local, transcendentals=rows * window * heads
        ),
        name="attend",
    )(bias, gain, raw, grad, kp, ko, kn, vp, vo, vn)

MESH = pl.DeviceIdType.MESH


def halving_orders(count, streams):
    bits = [1 << i for i in range(count.bit_length() - 1)]
    rest = bits[1:]
    orders = []
    for s in range(streams):
        turn = s % max(1, len(rest))
        orders.append(bits[:1] + rest[turn:] + rest[:turn])
    return orders


def subsets(bits):
    if not bits:
        return [0]
    tail = subsets(bits[1:])
    return [bits[0] | t for t in tail] + tail


def summed_kernel(count, streams, *refs):
    terms, outs = refs[:streams], refs[streams : 2 * streams]
    landed, send_sems, recv_sems = refs[2 * streams :]
    me = lax.axis_index("frame")
    rows = outs[0].shape[0]
    bits = [1 << i for i in range(count.bit_length() - 1)]
    shift = {b: b - 2 * b * (lax.div(me, b) % 2) for b in bits}

    barrier = pltpu.get_barrier_semaphore()
    for b in bits:
        pl.semaphore_signal(barrier, inc=1, device_id={"frame": me + shift[b]}, device_id_type=MESH)
    pl.semaphore_wait(barrier, len(bits))

    def block_of(term, relative):
        place = me
        for b in bits:
            if relative & b:
                place = place + shift[b]
        return term.at[pl.ds(pl.multiple_of(place * rows, rows), rows)]

    orders = halving_orders(count, streams)
    slots = [{} for _ in range(streams)]
    copies = [{} for _ in range(streams)]
    for s in range(streams):
        for k in range(len(bits)):
            for rest in subsets(orders[s][k + 1 :]):
                slots[s][k, rest] = len(slots[s])
    for k in range(len(bits)):
        lists = [subsets(orders[s][k + 1 :]) for s in range(streams)]
        for j in range(len(lists[0])):
            for s in range(streams):
                rest, bit = lists[s][j], orders[s][k]
                relative = rest | bit
                source = block_of(terms[s], relative)
                if k:
                    total = source[...].astype(jnp.float32)
                    for earlier in range(k):
                        copies[s][earlier, relative].wait_recv()
                        total += landed[s, slots[s][earlier, relative]].astype(jnp.float32)
                    slot = slots[s][k - 1, relative]
                    landed[s, slot] = total.astype(landed.dtype)
                    source = landed.at[s, slot]
                slot = slots[s][k, rest]
                copies[s][k, rest] = pltpu.make_async_remote_copy(
                    src_ref=source,
                    dst_ref=landed.at[s, slot],
                    send_sem=send_sems.at[s, slot],
                    recv_sem=recv_sems.at[s, slot],
                    device_id={"frame": me + shift[bit]},
                    device_id_type=MESH,
                )
                copies[s][k, rest].start()
    for s in range(streams):
        total = block_of(terms[s], 0)[...].astype(jnp.float32)
        for k in range(len(bits)):
            copies[s][k, 0].wait_recv()
            total += landed[s, slots[s][k, 0]].astype(jnp.float32)
        outs[s][...] = total
    for s in range(streams):
        for copy in copies[s].values():
            copy.wait_send()


def summed_over_frames(*terms):
    count, streams = lax.axis_size("frame"), len(terms)
    depth, local = terms[0].shape
    rows = depth // count
    vmem = pl.BlockSpec(memory_space=pltpu.VMEM)
    shape = jax.ShapeDtypeStruct((rows, local), jnp.float32)
    return pl.pallas_call(
        functools.partial(summed_kernel, count, streams),
        in_specs=[vmem] * streams,
        out_specs=(vmem,) * streams,
        out_shape=(shape,) * streams,
        scratch_shapes=[
            pltpu.VMEM((streams, count - 1, rows, local), terms[0].dtype),
            pltpu.SemaphoreType.DMA((streams, count - 1)),
            pltpu.SemaphoreType.DMA((streams, count - 1)),
        ],
        compiler_params=pltpu.CompilerParams(
            collective_id=0, has_side_effects=True, vmem_limit_bytes=40 * 1024 * 1024
        ),
        name="summed",
    )(*terms)


def per_device(hidden, qkv_weight, norm_gain, out_grad):
    gathered = lax.all_gather(hidden, "tensor", axis=0, tiled=True)
    rows = gathered.shape[0]
    half = rows // 2
    wq, wk, wv = (qkv_weight[:, i] for i in range(3))
    key_raw = dot32(gathered, wk)
    values = dot32(gathered, wv).astype(jnp.bfloat16)
    keys = key_norm(key_raw, norm_gain)
    kp, vp = (ppermute_by(a[rows - half :], "frame", 1) for a in (keys, values))
    kn, vn = (ppermute_by(a[:half], "frame", -1) for a in (keys, values))
    query_raw = dot32(gathered, wq)
    index, count = (lax.axis_index("frame"), lax.axis_size("frame"))
    bias = jnp.stack(
        [jnp.where(index > 0, 0.0, MASKED), jnp.where(index < count - 1, 0.0, MASKED)]
    ).astype(jnp.float32)
    attended, query_part, dk, dv, dkp, dvp, dkn, dvn = attend(
        bias, norm_gain, query_raw, out_grad, kp, keys, kn, vp, values, vn
    )
    from_next = [ppermute_by(a, "frame", -1) for a in (dkp, dvp)]
    from_prev = [ppermute_by(a, "frame", 1) for a in (dkn, dvn)]

    def weight_term(grads):
        term = lax.dot_general(
            gathered, grads, (((0,), (0,)), ((), ())), preferred_element_type=jnp.float32
        )
        return term.astype(jnp.bfloat16)

    def scattered(term):
        return lax.psum_scatter(term, "frame", scatter_dimension=0, tiled=True)

    query_weight = scattered(weight_term(query_part))
    key_part, value_part = key_back(
        dk, dv, from_prev[0], from_prev[1], from_next[0], from_next[1], key_raw, norm_gain
    )
    key_weight, value_weight = summed_over_frames(weight_term(key_part), weight_term(value_part))
    weight_grad = jnp.stack([query_weight.astype(jnp.float32), key_weight, value_weight], 1)
    return (attended, weight_grad)


def solution(mesh):
    placed = (P(("frame", "tensor"), None), P(None, None, "tensor"), P(), P("frame", "tensor"))
    return jax.shard_map(
        per_device,
        mesh=mesh,
        in_specs=placed,
        out_specs=(P("frame", "tensor"), P("frame", None, "tensor")),
        check_vma=False,
    )
```

```python
import functools
import math

import jax
import jax.numpy as jnp
from jax import lax
from jax.experimental import pallas as pl
from jax.experimental.pallas import tpu as pltpu
from jax.sharding import PartitionSpec as P

HEAD_DIM = 128
EPSILON = 1e-06
MASKED = -1e30
NT = (((1,), (1,)), ((), ()))


def ppermute_by(value, axis, steps):
    count = lax.axis_size(axis)
    initial, last = (max(0, -steps), min(count, count - steps))
    return lax.ppermute(value, axis, [(source, source + steps) for source in range(initial, last)])


def inverse_rms_of(raw):
    return lax.rsqrt(jnp.mean(raw * raw, axis=-1, keepdims=True) + EPSILON)


def norm_back(raw, inverse_rms, gain, grad):
    weighted = grad * gain
    inner = jnp.mean(raw * weighted, axis=-1, keepdims=True)
    return inverse_rms * weighted - raw * (inverse_rms * inverse_rms * inverse_rms) * inner


def dot32(left, right):
    return jnp.dot(left, right, preferred_element_type=jnp.float32)


def dot_nt(left, right):
    return lax.dot_general(left, right, NT, preferred_element_type=jnp.float32)


def key_back_kernel(dk_ref, dv_ref, pk_ref, pv_ref, nk_ref, nv_ref, raw_ref, gain_ref, kout_ref, vout_ref):
    half = pk_ref.shape[0]
    gain = gain_ref[1:2]
    for part, (k_edge, v_edge) in enumerate(((pk_ref, pv_ref), (nk_ref, nv_ref))):
        rows = pl.ds(part * half, half)
        raw = raw_ref[rows]
        grad = dk_ref[rows] + k_edge[...].astype(jnp.float32)
        kout_ref[rows] = norm_back(raw, inverse_rms_of(raw), gain, grad).astype(jnp.bfloat16)
        vout_ref[rows] = (dv_ref[rows] + v_edge[...].astype(jnp.float32)).astype(jnp.bfloat16)


def key_back(dk, dv, pk, pv, nk, nv, raw, gain):
    rows, local = dk.shape
    spec = pl.BlockSpec((rows, HEAD_DIM), lambda h: (0, h))
    edge = pl.BlockSpec((pk.shape[0], HEAD_DIM), lambda h: (0, h))
    shape = jax.ShapeDtypeStruct(dk.shape, jnp.bfloat16)
    return pl.pallas_call(
        key_back_kernel,
        grid=(local // HEAD_DIM,),
        in_specs=[spec, spec, edge, edge, edge, edge, spec, pl.BlockSpec(gain.shape, lambda h: (0, 0))],
        out_specs=(spec, spec),
        out_shape=(shape, shape),
        name="key_back",
    )(dk, dv, pk, pv, nk, nv, raw, gain)


def attend_kernel(
    bias_ref, gain_ref, raw_ref, grad_ref, kp_ref, ko_ref, kn_ref, vp_ref, vo_ref, vn_ref,
    att_ref, qpart_ref, dk_ref, dv_ref, dkp_ref, dvp_ref, dkn_ref, dvn_ref,
    kt, vt, score, prob_grad, weight, score_grad, dk_acc, dv_acc,
):
    half = kp_ref.shape[0]
    total = dk_acc.shape[0]
    step, last = pl.program_id(1), pl.num_programs(1) - 1
    factor = HEAD_DIM ** (-0.5)
    chunks = [
        (kp_ref, vp_ref, slice(0, half), bias_ref[0]),
        (ko_ref, vo_ref, slice(0, half), None),
        (ko_ref, vo_ref, slice(half, 2 * half), None),
        (kn_ref, vn_ref, slice(0, half), bias_ref[1]),
    ]

    @pl.when(step == 0)
    def _():
        for i, (k_ref, v_ref, rows, _) in enumerate(chunks):
            kt[:, i * half : (i + 1) * half] = k_ref[rows].T
            vt[:, i * half : (i + 1) * half] = v_ref[rows].T
        dk_acc[...] = jnp.zeros_like(dk_acc)
        dv_acc[...] = jnp.zeros_like(dv_acc)

    raw = raw_ref[...]
    gain = gain_ref[0:1]
    inverse_rms = inverse_rms_of(raw)
    query = (raw * inverse_rms * gain).astype(jnp.bfloat16)
    grad = grad_ref[...]
    peak = None
    for i, (k_ref, v_ref, rows, bias) in enumerate(chunks):
        place = slice(i * half, (i + 1) * half)
        s = dot_nt(k_ref[rows], query)
        if bias is not None:
            s = s + bias
        score[place] = s
        top = jnp.max(s, axis=0, keepdims=True)
        peak = top if peak is None else jnp.maximum(peak, top)
    norm = None
    scale = factor * math.log2(math.e)
    for i, (k_ref, v_ref, rows, _) in enumerate(chunks):
        place = slice(i * half, (i + 1) * half)
        raised = jnp.exp2((score[place] - peak) * scale)
        score[place] = raised
        part = jnp.sum(raised, axis=0, keepdims=True)
        norm = part if norm is None else norm + part
        prob_grad[place] = dot_nt(v_ref[rows], grad)
    inverse = 1.0 / norm
    attended = None
    for i in range(4):
        place = slice(i * half, (i + 1) * half)
        w = (score[place] * inverse).astype(jnp.bfloat16)
        weight[place] = w
        term = dot32(vt[:, place], w)
        attended = term if attended is None else attended + term
        dv_acc[place] += dot32(w, grad)
    attended = attended.T.astype(jnp.bfloat16)
    att_ref[...] = attended
    dots = jnp.sum((grad.astype(jnp.float32) * attended.astype(jnp.float32)).T, axis=0, keepdims=True)
    query_grad = None
    for i in range(4):
        place = slice(i * half, (i + 1) * half)
        ds = (weight[place].astype(jnp.float32) * (prob_grad[place] - dots)).astype(jnp.bfloat16)
        term = dot32(kt[:, place], ds)
        query_grad = term if query_grad is None else query_grad + term
        dk_acc[place] += dot32(ds, query)
    query_grad = query_grad.T * factor
    qpart_ref[...] = norm_back(raw, inverse_rms, gain, query_grad).astype(jnp.bfloat16)

    @pl.when(step == last)
    def _():
        dkp_ref[...] = (dk_acc[0:half] * factor).astype(jnp.bfloat16)
        dvp_ref[...] = dv_acc[0:half].astype(jnp.bfloat16)
        dk_ref[...] = dk_acc[half : 3 * half] * factor
        dv_ref[...] = dv_acc[half : 3 * half]
        dkn_ref[...] = (dk_acc[3 * half : total] * factor).astype(jnp.bfloat16)
        dvn_ref[...] = dv_acc[3 * half : total].astype(jnp.bfloat16)


def attend(bias, gain, raw, grad, kp, ko, kn, vp, vo, vn):
    rows, local = raw.shape
    heads, half = local // HEAD_DIM, rows // 2
    block = min(256, rows)
    by_row = pl.BlockSpec((block, HEAD_DIM), lambda h, j: (j, h))
    own = pl.BlockSpec((rows, HEAD_DIM), lambda h, j: (0, h))
    edge = pl.BlockSpec((half, HEAD_DIM), lambda h, j: (0, h))
    full = jax.ShapeDtypeStruct((rows, local), jnp.bfloat16)
    full32 = jax.ShapeDtypeStruct((rows, local), jnp.float32)
    edge_shape = jax.ShapeDtypeStruct((half, local), jnp.bfloat16)
    window = 2 * rows
    flops = 12 * rows * window * local
    return pl.pallas_call(
        attend_kernel,
        grid=(heads, rows // block),
        in_specs=[
            pl.BlockSpec(memory_space=pltpu.SMEM),
            pl.BlockSpec(gain.shape, lambda h, j: (0, 0)),
            by_row, by_row, edge, own, edge, edge, own, edge,
        ],
        out_specs=(by_row, by_row, own, own, edge, edge, edge, edge),
        out_shape=(full, full, full32, full32, edge_shape, edge_shape, edge_shape, edge_shape),
        scratch_shapes=[
            pltpu.VMEM((HEAD_DIM, window), jnp.bfloat16),
            pltpu.VMEM((HEAD_DIM, window), jnp.bfloat16),
            pltpu.VMEM((window, block), jnp.float32),
            pltpu.VMEM((window, block), jnp.float32),
            pltpu.VMEM((window, block), jnp.bfloat16),
            pltpu.VMEM((window, block), jnp.bfloat16),
            pltpu.VMEM((window, HEAD_DIM), jnp.float32),
            pltpu.VMEM((window, HEAD_DIM), jnp.float32),
        ],
        compiler_params=pltpu.CompilerParams(
            dimension_semantics=("arbitrary", "arbitrary"), vmem_limit_bytes=40 * 1024 * 1024
        ),
        cost_estimate=pl.CostEstimate(
            flops=flops, bytes_accessed=16 * rows * local, transcendentals=rows * window * heads
        ),
        name="attend",
    )(bias, gain, raw, grad, kp, ko, kn, vp, vo, vn)

MESH = pl.DeviceIdType.MESH


def halving_orders(count, streams):
    bits = [1 << i for i in range(count.bit_length() - 1)]
    rest = bits[1:]
    orders = []
    for s in range(streams):
        turn = s % max(1, len(rest))
        orders.append(bits[:1] + rest[turn:] + rest[:turn])
    return orders


def subsets(bits):
    if not bits:
        return [0]
    tail = subsets(bits[1:])
    return [bits[0] | t for t in tail] + tail


def summed_kernel(count, number, *refs):
    terms, outs = refs[:number], refs[number : 2 * number]
    landed, send_sems, recv_sems = refs[2 * number :]
    me = lax.axis_index("frame")
    full = outs[0].shape[0]
    streams, rows = 2 * number, full // 2
    bits = [1 << i for i in range(count.bit_length() - 1)]
    shift = {b: b - 2 * b * (lax.div(me, b) % 2) for b in bits}

    barrier = pltpu.get_barrier_semaphore()
    for b in bits:
        pl.semaphore_signal(barrier, inc=1, device_id={"frame": me + shift[b]}, device_id_type=MESH)
    pl.semaphore_wait(barrier, len(bits))

    def block_of(stream, relative):
        place = me
        for b in bits:
            if relative & b:
                place = place + shift[b]
        first = pl.multiple_of(place * full + (stream % 2) * rows, rows)
        return terms[stream // 2].at[pl.ds(first, rows)]

    orders = halving_orders(count, streams)
    slots = [{} for _ in range(streams)]
    copies = [{} for _ in range(streams)]
    for s in range(streams):
        for k in range(len(bits)):
            for rest in subsets(orders[s][k + 1 :]):
                slots[s][k, rest] = len(slots[s])
    for k in range(len(bits)):
        lists = [subsets(orders[s][k + 1 :]) for s in range(streams)]
        for j in range(len(lists[0])):
            for s in range(streams):
                rest, bit = lists[s][j], orders[s][k]
                relative = rest | bit
                source = block_of(s, relative)
                if k:
                    total = source[...].astype(jnp.float32)
                    for earlier in range(k):
                        copies[s][earlier, relative].wait_recv()
                        total += landed[s, slots[s][earlier, relative]].astype(jnp.float32)
                    slot = slots[s][k - 1, relative]
                    landed[s, slot] = total.astype(landed.dtype)
                    source = landed.at[s, slot]
                slot = slots[s][k, rest]
                copies[s][k, rest] = pltpu.make_async_remote_copy(
                    src_ref=source,
                    dst_ref=landed.at[s, slot],
                    send_sem=send_sems.at[s, slot],
                    recv_sem=recv_sems.at[s, slot],
                    device_id={"frame": me + shift[bit]},
                    device_id_type=MESH,
                )
                copies[s][k, rest].start()
    for s in range(streams):
        total = block_of(s, 0)[...].astype(jnp.float32)
        for k in range(len(bits)):
            copies[s][k, 0].wait_recv()
            total += landed[s, slots[s][k, 0]].astype(jnp.float32)
        outs[s // 2][(s % 2) * rows : (s % 2 + 1) * rows] = total
    for s in range(streams):
        for copy in copies[s].values():
            copy.wait_send()


def summed_over_frames(*terms):
    count, number = lax.axis_size("frame"), len(terms)
    depth, local = terms[0].shape
    rows = depth // count
    vmem = pl.BlockSpec(memory_space=pltpu.VMEM)
    shape = jax.ShapeDtypeStruct((rows, local), jnp.float32)
    return pl.pallas_call(
        functools.partial(summed_kernel, count, number),
        in_specs=[vmem] * number,
        out_specs=(vmem,) * number,
        out_shape=(shape,) * number,
        scratch_shapes=[
            pltpu.VMEM((2 * number, count - 1, rows // 2, local), terms[0].dtype),
            pltpu.SemaphoreType.DMA((2 * number, count - 1)),
            pltpu.SemaphoreType.DMA((2 * number, count - 1)),
        ],
        compiler_params=pltpu.CompilerParams(
            collective_id=0, has_side_effects=True, vmem_limit_bytes=40 * 1024 * 1024
        ),
        name="summed",
    )(*terms)


def project_kernel(
    count, gain_ref, hidden_ref, weight_hbm, gathered, query_raw, key_raw, keys, values,
    weight, weight_sems, send_sems, recv_sems,
):
    me = lax.axis_index("tensor")
    rows = hidden_ref.shape[0]
    has_left, has_right = me > 0, me < count - 1
    loads = [
        pltpu.make_async_copy(weight_hbm.at[i], weight.at[i], weight_sems.at[i]) for i in range(3)
    ]
    for load in loads:
        load.start()
    barrier = pltpu.get_barrier_semaphore()
    for there in (lax.rem(me + count - 1, count), lax.rem(me + 1, count)):
        pl.semaphore_signal(barrier, inc=1, device_id={"tensor": there}, device_id_type=MESH)
    pl.semaphore_wait(barrier, 2)

    def rows_of(shard):
        return pl.ds(pl.multiple_of(shard * rows, rows), rows)

    def copy_of(side, step, shard, source):
        return pltpu.make_async_remote_copy(
            src_ref=source,
            dst_ref=gathered.at[rows_of(shard)],
            send_sem=send_sems.at[side, step],
            recv_sem=recv_sems.at[side, step],
            device_id={"tensor": me + 1 - 2 * side},
            device_id_type=MESH,
        )

    for side, near in ((0, has_right), (1, has_left)):
        @pl.when(near)
        def _(side=side):
            copy_of(side, 0, me, hidden_ref).start()
    gathered[rows_of(me)] = hidden_ref[...]
    for load in loads:
        load.wait()

    def one_step(step, carry):
        @pl.when(step > 0)
        def _():
            for side, near in ((0, has_right), (1, has_left)):
                shard = me - step if side == 0 else me + step
                there = shard >= 0 if side == 0 else shard < count

                @pl.when(there)
                def _(side=side, shard=shard):
                    copy_of(side, step - 1, shard, gathered.at[rows_of(shard)]).wait_recv()

                @pl.when(there & near)
                def _(side=side, shard=shard):
                    copy_of(side, step, shard, gathered.at[rows_of(shard)]).start()

        def one_side(side, inner):
            shard = me - step + 2 * step * side

            @pl.when((shard >= 0) & (shard < count) & (step >= side))
            def _():
                place = rows_of(shard)
                tokens = gathered[place]
                raw = dot32(tokens, weight[1])
                key_raw[place] = raw
                for h in range(raw.shape[1] // HEAD_DIM):
                    columns = slice(h * HEAD_DIM, (h + 1) * HEAD_DIM)
                    head = raw[:, columns]
                    normed = head * inverse_rms_of(head) * gain_ref[1:2]
                    keys[place, columns] = normed.astype(keys.dtype)
                values[place] = dot32(tokens, weight[2]).astype(values.dtype)
                query_raw[place] = dot32(tokens, weight[0])

            return inner

        return lax.fori_loop(0, 2, one_side, carry)

    lax.fori_loop(0, count, one_step, 0)
    for step in range(count - 1):
        for side, near in ((0, has_right), (1, has_left)):
            shard = me - step if side == 0 else me + step
            there = shard >= 0 if side == 0 else shard < count

            @pl.when(there & near)
            def _(side=side, shard=shard, step=step):
                source = hidden_ref if step == 0 else gathered.at[rows_of(shard)]
                copy_of(side, step, shard, source).wait_send()


def project(hidden, qkv_weight, gain):
    count = lax.axis_size("tensor")
    rows, depth = hidden.shape
    local = qkv_weight.shape[2]
    total = rows * count
    vmem = pl.BlockSpec(memory_space=pltpu.VMEM)
    wide = jax.ShapeDtypeStruct((total, local), jnp.float32)
    narrow = jax.ShapeDtypeStruct((total, local), jnp.bfloat16)
    return pl.pallas_call(
        functools.partial(project_kernel, count),
        in_specs=[vmem, vmem, pl.BlockSpec(memory_space=pl.ANY)],
        out_specs=(vmem,) * 5,
        out_shape=(jax.ShapeDtypeStruct((total, depth), hidden.dtype), wide, wide, narrow, narrow),
        scratch_shapes=[
            pltpu.VMEM((3, depth, local), qkv_weight.dtype),
            pltpu.SemaphoreType.DMA((3,)),
            pltpu.SemaphoreType.DMA((2, count)),
            pltpu.SemaphoreType.DMA((2, count)),
        ],
        compiler_params=pltpu.CompilerParams(
            collective_id=1, has_side_effects=True, vmem_limit_bytes=50 * 1024 * 1024
        ),
        name="project",
    )(gain, hidden, jnp.transpose(qkv_weight, (1, 0, 2)))


def per_device(hidden, qkv_weight, norm_gain, out_grad):
    gathered, query_raw, key_raw, keys, values = project(hidden, qkv_weight, norm_gain)
    rows = gathered.shape[0]
    half = rows // 2
    kp, vp = (ppermute_by(a[rows - half :], "frame", 1) for a in (keys, values))
    kn, vn = (ppermute_by(a[:half], "frame", -1) for a in (keys, values))
    index, count = (lax.axis_index("frame"), lax.axis_size("frame"))
    bias = jnp.stack(
        [jnp.where(index > 0, 0.0, MASKED), jnp.where(index < count - 1, 0.0, MASKED)]
    ).astype(jnp.float32)
    attended, query_part, dk, dv, dkp, dvp, dkn, dvn = attend(
        bias, norm_gain, query_raw, out_grad, kp, keys, kn, vp, values, vn
    )
    from_next = [ppermute_by(a, "frame", -1) for a in (dkp, dvp)]
    from_prev = [ppermute_by(a, "frame", 1) for a in (dkn, dvn)]

    def weight_term(grads):
        term = lax.dot_general(
            gathered, grads, (((0,), (0,)), ((), ())), preferred_element_type=jnp.float32
        )
        return term.astype(jnp.bfloat16)

    key_part, value_part = key_back(
        dk, dv, from_prev[0], from_prev[1], from_next[0], from_next[1], key_raw, norm_gain
    )
    sums = summed_over_frames(*(weight_term(part) for part in (query_part, key_part, value_part)))
    weight_grad = jnp.stack(sums, 1)
    return (attended, weight_grad)


def solution(mesh):
    placed = (P(("frame", "tensor"), None), P(None, None, "tensor"), P(), P("frame", "tensor"))
    return jax.shard_map(
        per_device,
        mesh=mesh,
        in_specs=placed,
        out_specs=(P("frame", "tensor"), P("frame", None, "tensor")),
        check_vma=False,
    )
```

```python
import functools
import math

import jax
import jax.numpy as jnp
from jax import lax
from jax.experimental import pallas as pl
from jax.experimental.pallas import tpu as pltpu
from jax.sharding import PartitionSpec as P

HEAD_DIM = 128
EPSILON = 1e-06
MASKED = -1e30
NT = (((1,), (1,)), ((), ()))


def ppermute_by(value, axis, steps):
    count = lax.axis_size(axis)
    initial, last = (max(0, -steps), min(count, count - steps))
    return lax.ppermute(value, axis, [(source, source + steps) for source in range(initial, last)])


def inverse_rms_of(raw):
    return lax.rsqrt(jnp.mean(raw * raw, axis=-1, keepdims=True) + EPSILON)


def norm_back(raw, inverse_rms, gain, grad):
    weighted = grad * gain
    inner = jnp.mean(raw * weighted, axis=-1, keepdims=True)
    return inverse_rms * weighted - raw * (inverse_rms * inverse_rms * inverse_rms) * inner


def dot32(left, right):
    return jnp.dot(left, right, preferred_element_type=jnp.float32)


def dot_nt(left, right):
    return lax.dot_general(left, right, NT, preferred_element_type=jnp.float32)


def key_back_kernel(dk_ref, dv_ref, pk_ref, pv_ref, nk_ref, nv_ref, raw_ref, gain_ref, kout_ref, vout_ref):
    half = pk_ref.shape[0]
    gain = gain_ref[1:2]
    for part, (k_edge, v_edge) in enumerate(((pk_ref, pv_ref), (nk_ref, nv_ref))):
        rows = pl.ds(part * half, half)
        raw = raw_ref[rows]
        grad = dk_ref[rows] + k_edge[...].astype(jnp.float32)
        kout_ref[rows] = norm_back(raw, inverse_rms_of(raw), gain, grad).astype(jnp.bfloat16)
        vout_ref[rows] = (dv_ref[rows] + v_edge[...].astype(jnp.float32)).astype(jnp.bfloat16)


def key_back(dk, dv, pk, pv, nk, nv, raw, gain):
    rows, local = dk.shape
    spec = pl.BlockSpec((rows, HEAD_DIM), lambda h: (0, h))
    edge = pl.BlockSpec((pk.shape[0], HEAD_DIM), lambda h: (0, h))
    shape = jax.ShapeDtypeStruct(dk.shape, jnp.bfloat16)
    return pl.pallas_call(
        key_back_kernel,
        grid=(local // HEAD_DIM,),
        in_specs=[spec, spec, edge, edge, edge, edge, spec, pl.BlockSpec(gain.shape, lambda h: (0, 0))],
        out_specs=(spec, spec),
        out_shape=(shape, shape),
        name="key_back",
    )(dk, dv, pk, pv, nk, nv, raw, gain)


def attend_kernel(
    bias_ref, gain_ref, raw_ref, grad_ref, kp_ref, ko_ref, kn_ref, vp_ref, vo_ref, vn_ref,
    att_ref, qpart_ref, dk_ref, dv_ref, dkp_ref, dvp_ref, dkn_ref, dvn_ref,
    kt, vt, score, prob_grad, weight, dk_acc, dv_acc,
):
    half = kp_ref.shape[0]
    total = dk_acc.shape[0]
    step, last = pl.program_id(1), pl.num_programs(1) - 1
    factor = HEAD_DIM ** (-0.5)
    chunks = [
        (kp_ref, vp_ref, slice(0, half), bias_ref[0]),
        (ko_ref, vo_ref, slice(0, half), None),
        (ko_ref, vo_ref, slice(half, 2 * half), None),
        (kn_ref, vn_ref, slice(0, half), bias_ref[1]),
    ]

    @pl.when(step == 0)
    def _():
        for i, (k_ref, v_ref, rows, _) in enumerate(chunks):
            kt[:, i * half : (i + 1) * half] = k_ref[rows].T
            vt[:, i * half : (i + 1) * half] = v_ref[rows].T
        dk_acc[...] = jnp.zeros_like(dk_acc)
        dv_acc[...] = jnp.zeros_like(dv_acc)

    raw = raw_ref[...]
    gain = gain_ref[0:1]
    inverse_rms = inverse_rms_of(raw)
    query = (raw * inverse_rms * gain).astype(jnp.bfloat16)
    grad = grad_ref[...]
    peak = None
    for i, (k_ref, v_ref, rows, bias) in enumerate(chunks):
        place = slice(i * half, (i + 1) * half)
        s = dot_nt(k_ref[rows], query)
        if bias is not None:
            s = s + bias
        score[place] = s
        top = jnp.max(s, axis=0, keepdims=True)
        peak = top if peak is None else jnp.maximum(peak, top)
    norm = None
    scale = factor * math.log2(math.e)
    for i, (k_ref, v_ref, rows, _) in enumerate(chunks):
        place = slice(i * half, (i + 1) * half)
        raised = jnp.exp2((score[place] - peak) * scale)
        score[place] = raised
        part = jnp.sum(raised, axis=0, keepdims=True)
        norm = part if norm is None else norm + part
        prob_grad[place] = dot_nt(v_ref[rows], grad)
    inverse = 1.0 / norm
    attended = None
    for i in range(4):
        place = slice(i * half, (i + 1) * half)
        w = (score[place] * inverse).astype(jnp.bfloat16)
        weight[place] = w
        term = dot32(vt[:, place], w)
        attended = term if attended is None else attended + term
        dv_acc[place] += dot32(w, grad)
    attended = attended.T.astype(jnp.bfloat16)
    att_ref[...] = attended
    dots = jnp.sum((grad.astype(jnp.float32) * attended.astype(jnp.float32)).T, axis=0, keepdims=True)
    query_grad = None
    for i in range(4):
        place = slice(i * half, (i + 1) * half)
        ds = (weight[place].astype(jnp.float32) * (prob_grad[place] - dots)).astype(jnp.bfloat16)
        term = dot32(kt[:, place], ds)
        query_grad = term if query_grad is None else query_grad + term
        dk_acc[place] += dot32(ds, query)
    query_grad = query_grad.T * factor
    qpart_ref[...] = norm_back(raw, inverse_rms, gain, query_grad).astype(jnp.bfloat16)

    @pl.when(step == last)
    def _():
        dkp_ref[...] = (dk_acc[0:half] * factor).astype(jnp.bfloat16)
        dvp_ref[...] = dv_acc[0:half].astype(jnp.bfloat16)
        dk_ref[...] = dk_acc[half : 3 * half] * factor
        dv_ref[...] = dv_acc[half : 3 * half]
        dkn_ref[...] = (dk_acc[3 * half : total] * factor).astype(jnp.bfloat16)
        dvn_ref[...] = dv_acc[3 * half : total].astype(jnp.bfloat16)


def attend(bias, gain, raw, grad, kp, ko, kn, vp, vo, vn):
    rows, local = raw.shape
    heads, half = local // HEAD_DIM, rows // 2
    block = min(512, rows)
    by_row = pl.BlockSpec((block, HEAD_DIM), lambda h, j: (j, h))
    own = pl.BlockSpec((rows, HEAD_DIM), lambda h, j: (0, h))
    edge = pl.BlockSpec((half, HEAD_DIM), lambda h, j: (0, h))
    full = jax.ShapeDtypeStruct((rows, local), jnp.bfloat16)
    full32 = jax.ShapeDtypeStruct((rows, local), jnp.float32)
    edge_shape = jax.ShapeDtypeStruct((half, local), jnp.bfloat16)
    window = 2 * rows
    flops = 12 * rows * window * local
    return pl.pallas_call(
        attend_kernel,
        grid=(heads, rows // block),
        in_specs=[
            pl.BlockSpec(memory_space=pltpu.SMEM),
            pl.BlockSpec(gain.shape, lambda h, j: (0, 0)),
            by_row, by_row, edge, own, edge, edge, own, edge,
        ],
        out_specs=(by_row, by_row, own, own, edge, edge, edge, edge),
        out_shape=(full, full, full32, full32, edge_shape, edge_shape, edge_shape, edge_shape),
        scratch_shapes=[
            pltpu.VMEM((HEAD_DIM, window), jnp.bfloat16),
            pltpu.VMEM((HEAD_DIM, window), jnp.bfloat16),
            pltpu.VMEM((window, block), jnp.float32),
            pltpu.VMEM((window, block), jnp.float32),
            pltpu.VMEM((window, block), jnp.bfloat16),
            pltpu.VMEM((window, HEAD_DIM), jnp.float32),
            pltpu.VMEM((window, HEAD_DIM), jnp.float32),
        ],
        compiler_params=pltpu.CompilerParams(
            dimension_semantics=("arbitrary", "arbitrary"), vmem_limit_bytes=40 * 1024 * 1024
        ),
        cost_estimate=pl.CostEstimate(
            flops=flops, bytes_accessed=16 * rows * local, transcendentals=rows * window * heads
        ),
        name="attend",
    )(bias, gain, raw, grad, kp, ko, kn, vp, vo, vn)

MESH = pl.DeviceIdType.MESH


def halving_orders(count, streams):
    bits = [1 << i for i in range(count.bit_length() - 1)]
    rest = bits[1:]
    orders = []
    for s in range(streams):
        turn = s % max(1, len(rest))
        orders.append(bits[:1] + rest[turn:] + rest[:turn])
    return orders


def subsets(bits):
    if not bits:
        return [0]
    tail = subsets(bits[1:])
    return [bits[0] | t for t in tail] + tail


def summed_kernel(count, number, *refs):
    terms, outs = refs[:number], refs[number : 2 * number]
    landed, send_sems, recv_sems = refs[2 * number :]
    me = lax.axis_index("frame")
    full = outs[0].shape[0]
    streams, rows = 2 * number, full // 2
    bits = [1 << i for i in range(count.bit_length() - 1)]
    shift = {b: b - 2 * b * (lax.div(me, b) % 2) for b in bits}

    barrier = pltpu.get_barrier_semaphore()
    for b in bits:
        pl.semaphore_signal(barrier, inc=1, device_id={"frame": me + shift[b]}, device_id_type=MESH)
    pl.semaphore_wait(barrier, len(bits))

    def block_of(stream, relative):
        place = me
        for b in bits:
            if relative & b:
                place = place + shift[b]
        first = pl.multiple_of(place * full + (stream % 2) * rows, rows)
        return terms[stream // 2].at[pl.ds(first, rows)]

    orders = halving_orders(count, streams)
    slots = [{} for _ in range(streams)]
    copies = [{} for _ in range(streams)]
    for s in range(streams):
        for k in range(len(bits)):
            for rest in subsets(orders[s][k + 1 :]):
                slots[s][k, rest] = len(slots[s])
    for k in range(len(bits)):
        lists = [subsets(orders[s][k + 1 :]) for s in range(streams)]
        for j in range(len(lists[0])):
            for s in range(streams):
                rest, bit = lists[s][j], orders[s][k]
                relative = rest | bit
                source = block_of(s, relative)
                if k:
                    total = source[...].astype(jnp.float32)
                    for earlier in range(k):
                        copies[s][earlier, relative].wait_recv()
                        total += landed[s, slots[s][earlier, relative]].astype(jnp.float32)
                    slot = slots[s][k - 1, relative]
                    landed[s, slot] = total.astype(landed.dtype)
                    source = landed.at[s, slot]
                slot = slots[s][k, rest]
                copies[s][k, rest] = pltpu.make_async_remote_copy(
                    src_ref=source,
                    dst_ref=landed.at[s, slot],
                    send_sem=send_sems.at[s, slot],
                    recv_sem=recv_sems.at[s, slot],
                    device_id={"frame": me + shift[bit]},
                    device_id_type=MESH,
                )
                copies[s][k, rest].start()
    for s in range(streams):
        total = block_of(s, 0)[...].astype(jnp.float32)
        for k in range(len(bits)):
            copies[s][k, 0].wait_recv()
            total += landed[s, slots[s][k, 0]].astype(jnp.float32)
        outs[s // 2][(s % 2) * rows : (s % 2 + 1) * rows] = total
    for s in range(streams):
        for copy in copies[s].values():
            copy.wait_send()


def summed_over_frames(*terms):
    count, number = lax.axis_size("frame"), len(terms)
    depth, local = terms[0].shape
    rows = depth // count
    vmem = pl.BlockSpec(memory_space=pltpu.VMEM)
    shape = jax.ShapeDtypeStruct((rows, local), jnp.float32)
    return pl.pallas_call(
        functools.partial(summed_kernel, count, number),
        in_specs=[vmem] * number,
        out_specs=(vmem,) * number,
        out_shape=(shape,) * number,
        scratch_shapes=[
            pltpu.VMEM((2 * number, count - 1, rows // 2, local), terms[0].dtype),
            pltpu.SemaphoreType.DMA((2 * number, count - 1)),
            pltpu.SemaphoreType.DMA((2 * number, count - 1)),
        ],
        compiler_params=pltpu.CompilerParams(
            collective_id=0, has_side_effects=True, vmem_limit_bytes=40 * 1024 * 1024
        ),
        name="summed",
    )(*terms)


def project_kernel(
    count, gain_ref, hidden_ref, weight_hbm, gathered, query_raw, key_raw, keys, values,
    weight, weight_sems, send_sems, recv_sems,
):
    me = lax.axis_index("tensor")
    rows = hidden_ref.shape[0]
    has_left, has_right = me > 0, me < count - 1
    loads = [
        pltpu.make_async_copy(weight_hbm.at[i], weight.at[i], weight_sems.at[i]) for i in range(3)
    ]
    for load in loads:
        load.start()
    barrier = pltpu.get_barrier_semaphore()
    for there in (lax.rem(me + count - 1, count), lax.rem(me + 1, count)):
        pl.semaphore_signal(barrier, inc=1, device_id={"tensor": there}, device_id_type=MESH)
    pl.semaphore_wait(barrier, 2)

    def rows_of(shard):
        return pl.ds(pl.multiple_of(shard * rows, rows), rows)

    def copy_of(side, step, shard, source):
        return pltpu.make_async_remote_copy(
            src_ref=source,
            dst_ref=gathered.at[rows_of(shard)],
            send_sem=send_sems.at[side, step],
            recv_sem=recv_sems.at[side, step],
            device_id={"tensor": me + 1 - 2 * side},
            device_id_type=MESH,
        )

    for side, near in ((0, has_right), (1, has_left)):
        @pl.when(near)
        def _(side=side):
            copy_of(side, 0, me, hidden_ref).start()
    gathered[rows_of(me)] = hidden_ref[...]
    for load in loads:
        load.wait()

    def one_step(step, carry):
        @pl.when(step > 0)
        def _():
            for side, near in ((0, has_right), (1, has_left)):
                shard = me - step if side == 0 else me + step
                there = shard >= 0 if side == 0 else shard < count

                @pl.when(there)
                def _(side=side, shard=shard):
                    copy_of(side, step - 1, shard, gathered.at[rows_of(shard)]).wait_recv()

                @pl.when(there & near)
                def _(side=side, shard=shard):
                    copy_of(side, step, shard, gathered.at[rows_of(shard)]).start()

        def one_side(side, inner):
            shard = me - step + 2 * step * side

            @pl.when((shard >= 0) & (shard < count) & (step >= side))
            def _():
                place = rows_of(shard)
                tokens = gathered[place]
                raw = dot32(tokens, weight[1])
                key_raw[place] = raw
                for h in range(raw.shape[1] // HEAD_DIM):
                    columns = slice(h * HEAD_DIM, (h + 1) * HEAD_DIM)
                    head = raw[:, columns]
                    normed = head * inverse_rms_of(head) * gain_ref[1:2]
                    keys[place, columns] = normed.astype(keys.dtype)
                values[place] = dot32(tokens, weight[2]).astype(values.dtype)
                query_raw[place] = dot32(tokens, weight[0])

            return inner

        return lax.fori_loop(0, 2, one_side, carry)

    lax.fori_loop(0, count, one_step, 0)
    for step in range(count - 1):
        for side, near in ((0, has_right), (1, has_left)):
            shard = me - step if side == 0 else me + step
            there = shard >= 0 if side == 0 else shard < count

            @pl.when(there & near)
            def _(side=side, shard=shard, step=step):
                source = hidden_ref if step == 0 else gathered.at[rows_of(shard)]
                copy_of(side, step, shard, source).wait_send()


def project(hidden, qkv_weight, gain):
    count = lax.axis_size("tensor")
    rows, depth = hidden.shape
    local = qkv_weight.shape[2]
    total = rows * count
    vmem = pl.BlockSpec(memory_space=pltpu.VMEM)
    wide = jax.ShapeDtypeStruct((total, local), jnp.float32)
    narrow = jax.ShapeDtypeStruct((total, local), jnp.bfloat16)
    return pl.pallas_call(
        functools.partial(project_kernel, count),
        in_specs=[vmem, vmem, pl.BlockSpec(memory_space=pl.ANY)],
        out_specs=(vmem,) * 5,
        out_shape=(jax.ShapeDtypeStruct((total, depth), hidden.dtype), wide, wide, narrow, narrow),
        scratch_shapes=[
            pltpu.VMEM((3, depth, local), qkv_weight.dtype),
            pltpu.SemaphoreType.DMA((3,)),
            pltpu.SemaphoreType.DMA((2, count)),
            pltpu.SemaphoreType.DMA((2, count)),
        ],
        compiler_params=pltpu.CompilerParams(
            collective_id=1, has_side_effects=True, vmem_limit_bytes=50 * 1024 * 1024
        ),
        name="project",
    )(gain, hidden, jnp.transpose(qkv_weight, (1, 0, 2)))


def per_device(hidden, qkv_weight, norm_gain, out_grad):
    gathered, query_raw, key_raw, keys, values = project(hidden, qkv_weight, norm_gain)
    rows = gathered.shape[0]
    half = rows // 2
    kp, vp = (ppermute_by(a[rows - half :], "frame", 1) for a in (keys, values))
    kn, vn = (ppermute_by(a[:half], "frame", -1) for a in (keys, values))
    index, count = (lax.axis_index("frame"), lax.axis_size("frame"))
    bias = jnp.stack(
        [jnp.where(index > 0, 0.0, MASKED), jnp.where(index < count - 1, 0.0, MASKED)]
    ).astype(jnp.float32)
    attended, query_part, dk, dv, dkp, dvp, dkn, dvn = attend(
        bias, norm_gain, query_raw, out_grad, kp, keys, kn, vp, values, vn
    )
    from_next = [ppermute_by(a, "frame", -1) for a in (dkp, dvp)]
    from_prev = [ppermute_by(a, "frame", 1) for a in (dkn, dvn)]

    def weight_term(grads):
        term = lax.dot_general(
            gathered, grads, (((0,), (0,)), ((), ())), preferred_element_type=jnp.float32
        )
        return term.astype(jnp.bfloat16)

    key_part, value_part = key_back(
        dk, dv, from_prev[0], from_prev[1], from_next[0], from_next[1], key_raw, norm_gain
    )
    sums = summed_over_frames(*(weight_term(part) for part in (query_part, key_part, value_part)))
    weight_grad = jnp.stack(sums, 1)
    return (attended, weight_grad)


def solution(mesh):
    placed = (P(("frame", "tensor"), None), P(None, None, "tensor"), P(), P("frame", "tensor"))
    return jax.shard_map(
        per_device,
        mesh=mesh,
        in_specs=placed,
        out_specs=(P("frame", "tensor"), P("frame", None, "tensor")),
        check_vma=False,
    )
```
